32 devices in a mesh: region: 2 (over x), rows: 8 (over z, y), section: 2 (over core).
Axes of the slice: x: 2, y: 2, z: 4, core: 2. Of those that a mesh axis runs over, the one named last changes fastest.
Arguments:
- transitions: float32 [4, 4, 4096, 4096], P(('region', 'section'), None, 'rows'), parts along dimension 0, may hold values from 0 to 1, as said below
- gain: float32 [4, 4, 4096], P(('region', 'section'), None, 'rows'), parts along dimension 0, may hold values from 0 to 1
- cost: float32 [4, 4, 8], P(('region', 'section')), parts along dimension 0, may hold values from 0 to 1
- price_class: int32 [2048], P('region'), parts along dimension 0, may hold values from 0 to 7
- terminal: float32 [8192, 1024], P(('region', 'rows')), parts along dimension 0, may hold values from 0.5 to 3.5
Outputs:
- values: float32 [4, 4096, 1024], P(('region', 'section'), 'rows'), parts along dimension 0
The draws below stay inside these ranges and needn't reach their ends.
There are 2 independent parts, one for each index of `region`. The reference program is written for one: setup_inputs(seed, part) draws one part's arguments, and reference() takes and returns one part's arrays. A program takes and returns all parts, laid end to end along the dimension named above; each array names one. Nothing has to cross between parts.
Inputs may be any that keep to these rules, and one draw needn't show every extreme that they name: `transitions`: entries are nonnegative.
All inputs are finite; a program needn't handle non-finite values.
Results may differ from the reference program's by a relative error of at most 0.0001.
Values sent between devices are 32-bit elements; how exact they have to be, the bound alone decides.
No kernel may reach another device: no remote copies, remote signals or barrier semaphores. Data moves between devices by JAX's collectives and lax.ppermute only.
A program may use at most 128 MiB of HBM per device.

```python
import jax
import jax.numpy as jnp
from jax import lax

STATES = 4096
ACTIONS = 4
PRICES = 8
SCEN = 1024
SECTIONS = 2


def draw_transitions(key, part):
    key_stay = jax.random.fold_in(key, 101)
    key_mass = jax.random.fold_in(key, 202)
    full_shape = (SECTIONS, ACTIONS, STATES, STATES)
    stay = jax.random.uniform(key_stay, (SECTIONS, ACTIONS, STATES, 1), jnp.float32, 0.3, 0.7)
    normal_draw = jnp.clip(jax.random.normal(key_mass, full_shape, jnp.float32), -4.0, 4.0)
    weight_mass = jnp.exp(1.5 * normal_draw - 1.125)
    rows_index = lax.broadcasted_iota(jnp.int32, full_shape, 2)
    cols_index = lax.broadcasted_iota(jnp.int32, full_shape, 3)
    diagonal = jnp.where(rows_index == cols_index, stay, 0.0)
    return diagonal + (1.0 - stay) * weight_mass / STATES


def place_ends(array, key, smallest, largest):
    longest = array.shape.index(max(array.shape))
    spots = []
    for shift in (0, 1):
        where = [jax.random.randint(jax.random.fold_in(key, axis), (), 0, length) for axis, length in enumerate(array.shape)]
        where[longest] = (where[longest] + shift) % array.shape[longest]
        spots.append(tuple(where))
    return array.at[spots[0]].set(smallest).at[spots[1]].set(largest)


def block_levels(rng, shape, cuts, smallest, high):
    level, own = 1.0, jax.random.fold_in(rng, 6)
    for dim, parts in cuts:
        steps = jnp.exp(jax.random.uniform(jax.random.fold_in(own, dim), (parts,), jnp.float32, smallest / len(cuts), high / len(cuts)))
        level = level * jnp.repeat(steps, shape[dim] // parts).reshape([-1 if axis == dim else 1 for axis in range(len(shape))])
    return level


def setup_inputs(seed: int = 0, part: int = 0) -> dict:
    seeds = jax.random.split(jax.random.key(seed), 6)
    part_splits = jax.random.split(jax.random.fold_in(seeds[5], part), 6)
    transitions = draw_transitions(jax.random.fold_in(jax.random.fold_in(seeds[5], part), 71), part)
    gain = jnp.clip(1.0 * jax.random.uniform(part_splits[1], (SECTIONS, ACTIONS, STATES), jnp.float32) ** block_levels(part_splits[1], (SECTIONS, ACTIONS, STATES), ((0, 2), (2, 8)), -0.2, 0.2), 0.0, 1.0)
    cost = jnp.clip(1.0 * jax.random.uniform(part_splits[2], (SECTIONS, ACTIONS, PRICES), jnp.float32) ** block_levels(part_splits[2], (SECTIONS, ACTIONS, PRICES), ((0, 2),), -0.2, 0.2), 0.0, 1.0)
    price_class = place_ends(jax.random.randint(part_splits[3], (SCEN,), 0, PRICES), jax.random.fold_in(part_splits[3], 1), 0, PRICES - 1).astype(jnp.int32)
    terminal = jnp.clip(0.5 + 3.0 * jax.random.uniform(part_splits[4], (STATES, SCEN), jnp.float32) ** block_levels(part_splits[4], (STATES, SCEN), ((0, 8),), -0.2, 0.2), 0.5, 3.5)
    return dict(transitions=transitions, gain=gain, cost=cost, price_class=price_class, terminal=terminal)


def reference(transitions, gain, cost, price_class, terminal):
    levels = jnp.arange(PRICES, dtype=jnp.int32)
    onehot = (price_class[None, :] == levels[:, None]).astype(terminal.dtype)
    values_now = terminal
    collected = []
    for section_index in range(SECTIONS - 1, -1, -1):
        charge = jnp.dot(cost[section_index], onehot, precision=lax.Precision.HIGHEST)
        best_value = None
        for action_index in range(ACTIONS):
            action_value = jnp.dot(transitions[section_index, action_index], values_now, precision=lax.Precision.HIGHEST)
            action_value = action_value + gain[section_index, action_index][:, None] - charge[action_index][None, :]
            best_value = action_value if best_value is None else jnp.maximum(best_value, action_value)
        values_now = best_value
        collected.append(values_now)
    return jnp.stack(collected[::-1], 0)
```

```python
import functools

import jax
import jax.numpy as jnp
from jax import lax
from jax.experimental import pallas as pl
from jax.experimental.pallas import tpu as pltpu
from jax.sharding import PartitionSpec as P

WIDTHS = (1, 1)
MINOR = 2
WINDOW = 2


def after(value, *others):
    return lax.optimization_barrier((value, *others))[0]


def split(x):
    high = x.astype(jnp.bfloat16)
    return high, (x - high.astype(jnp.float32)).astype(jnp.bfloat16)


def part_kernel(count, tile, first, last, first_col, order, kernel_hbm, *rest):
    gain_ref, charge_ref = rest[:2] if last else (None, None)
    rest = rest[2:] if last else rest
    blocks, rest = rest[:count], rest[count:]
    total_hbm, rest = (None, rest) if first else (rest[0], rest[1:])
    if last:
        batch_hbm, result_hbm, *rest = rest[-12:]
    else:
        sum_hbm, *rest = rest
    staged, x_high, x_low, tiles, totals, outs, x_sem, t_sem, a_sem, o_sem = rest
    actions, rows, _ = kernel_hbm.shape
    depth, width = blocks[0].shape
    tile_count = rows // tile

    def stage_copy(i):
        return pltpu.make_async_copy(blocks[i], staged.at[i], x_sem.at[i])

    def in_copies(t, slot):
        here = pl.ds(pl.multiple_of(t * tile, tile), tile)
        copies = [
            pltpu.make_async_copy(
                kernel_hbm.at[:, here, pl.ds(pl.multiple_of(order[1 + i] * depth, depth), depth)],
                tiles.at[slot, :, :, pl.ds(i * depth, depth)],
                t_sem.at[slot, i],
            )
            for i in range(count)
        ]
        if not first:
            copies.append(pltpu.make_async_copy(total_hbm.at[:, here, :], totals.at[slot], a_sem.at[slot]))
        return copies

    def out_copies(t, slot):
        here = pl.ds(pl.multiple_of(t * tile, tile), tile)
        if not last:
            return [pltpu.make_async_copy(outs.at[slot], sum_hbm.at[:, here, :], o_sem.at[slot, 0])]
        return [
            pltpu.make_async_copy(outs.at[slot, 0], batch_hbm.at[here, :], o_sem.at[slot, 0]),
            pltpu.make_async_copy(outs.at[slot, 0], result_hbm.at[0, here, pl.ds(first_col, width)], o_sem.at[slot, 1]),
        ]

    @pl.when(order[0] == 1)
    def _():
        for i in range(count):
            stage_copy(i).start()
        for copy in in_copies(0, 0):
            copy.start()
        for i in range(count):
            stage_copy(i).wait()
            high, low = split(staged[i])
            x_high[pl.ds(i * depth, depth), :] = high
            x_low[pl.ds(i * depth, depth), :] = low

        @pl.loop(0, tile_count)
        def _(t):
            slot = lax.rem(t, 2)

            @pl.when(t + 1 < tile_count)
            def _():
                for copy in in_copies(t + 1, 1 - slot):
                    copy.start()

            for copy in in_copies(t, slot):
                copy.wait()

            @pl.when(t >= 2)
            def _():
                for copy in out_copies(t - 2, slot):
                    copy.wait()

            high, low = split(tiles[slot].reshape(actions * tile, count * depth))
            dot = functools.partial(jnp.dot, preferred_element_type=jnp.float32)
            summed = dot(high, x_high[...]) + (dot(high, x_low[...]) + dot(low, x_high[...]))
            summed = summed.reshape(actions, tile, width)
            if not first:
                summed = summed + totals[slot]
            if not last:
                outs[slot] = summed
            else:
                gains = gain_ref[pl.ds(pl.multiple_of(t * tile, tile), tile), :]
                best = None
                for a in range(actions):
                    here = summed[a] + gains[:, a : a + 1] - charge_ref[a : a + 1, :]
                    best = here if best is None else jnp.maximum(best, here)
                outs[slot, 0] = best
            for copy in out_copies(t, slot):
                copy.start()

        for t in range(max(tile_count - 2, 0), tile_count):
            for copy in out_copies(t, t % 2):
                copy.wait()


def part(order, kernel, gains, charge, blocks, total, result, first_col, last):
    first = total is None
    fresh = isinstance(result, tuple)
    actions, rows, _ = kernel.shape
    count = len(blocks)
    depth, width = blocks[0].shape
    tile = min(rows, 128)
    hbm = pl.BlockSpec(memory_space=pl.ANY)
    vmem = pl.BlockSpec(memory_space=pltpu.VMEM)
    operands, specs = [order, kernel], [pl.BlockSpec(memory_space=pltpu.SMEM), hbm]
    if last:
        operands += [gains, charge]
        specs += [vmem, vmem]
    operands += blocks
    specs += [hbm] * count
    if not first:
        operands.append(total)
        specs.append(hbm)
    aliases = {}
    if last:
        if not fresh:
            aliases = {len(operands): 1}
            operands.append(result)
            specs.append(hbm)
        out_shape = (
            jax.ShapeDtypeStruct((rows, width), jnp.float32),
            jax.ShapeDtypeStruct(result if fresh else result.shape, jnp.float32),
        )
    else:
        out_shape = (jax.ShapeDtypeStruct((actions, rows, width), jnp.float32),)
    return pl.pallas_call(
        functools.partial(part_kernel, count, tile, first, last, first_col),
        out_shape=out_shape,
        in_specs=specs,
        out_specs=tuple([hbm] * len(out_shape)),
        scratch_shapes=[
            pltpu.VMEM((count, depth, width), jnp.float32),
            pltpu.VMEM((count * depth, width), jnp.bfloat16),
            pltpu.VMEM((count * depth, width), jnp.bfloat16),
            pltpu.VMEM((2, actions, tile, count * depth), jnp.float32),
            pltpu.VMEM((2, actions, tile, width) if not first else (2, 1, 8, 128), jnp.float32),
            pltpu.VMEM((2, 1 if last else actions, tile, width), jnp.float32),
            pltpu.SemaphoreType.DMA((count,)),
            pltpu.SemaphoreType.DMA((2, count)),
            pltpu.SemaphoreType.DMA((2,)),
            pltpu.SemaphoreType.DMA((2, 2)),
        ],
        input_output_aliases=aliases,
        compiler_params=pltpu.CompilerParams(vmem_limit_bytes=40 * 1024 * 1024),
        cost_estimate=pl.CostEstimate(
            flops=6 * actions * rows * count * depth * width,
            bytes_accessed=4 * actions * rows * count * depth,
            transcendentals=0,
        ),
        name="part",
    )(*operands)


class Lane:
    def __init__(self):
        self.done = []

    def send(self, value, pairs, *behind):
        behind = list(behind)
        if len(self.done) >= WINDOW:
            behind.append(self.done[-WINDOW])
        if behind:
            value = after(value, *behind)
        value = lax.ppermute(value, ("rows", "section"), pairs)
        self.done.append(value)
        return value


def shards(transitions, gain, cost, price_class, terminal):
    groups = lax.axis_size("section")
    my_group = lax.axis_index("section")
    row_count = lax.axis_size("rows")
    minor = MINOR if row_count % MINOR == 0 else 1
    major = row_count // minor
    me = lax.axis_index("rows")
    z, y = me // minor, me % minor

    def pairs(by, across, begin, target):
        return [
            (
                (i * minor + j) * groups + begin,
                ((i + by) % major * minor + (j + across) % minor) * groups + target,
            )
            for i in range(major)
            for j in range(minor)
        ]

    kernel = transitions[0]
    rows_here = kernel.shape[1]
    scenarios = terminal.shape[1]
    levels = jnp.arange(cost.shape[2], dtype=jnp.int32)
    onehot = price_class[None, :] == levels[:, None]
    charge = jnp.sum(jnp.where(onehot[None], cost[0][:, :, None], 0.0), axis=1)
    gains = gain[0].T
    bounds = [0]
    for share in WIDTHS:
        bounds.append(bounds[-1] + scenarios * share // sum(WIDTHS))
    spans = list(zip(bounds[:-1], bounds[1:]))
    result = (1, rows_here, scenarios)
    batches = [terminal[:, a:b] for a, b in spans]
    shifts = [0, 1, *([major - 1] if major > 2 else []), *range(2, major - 1)]
    for group in range(groups - 1, -1, -1):
        live = (my_group == group).astype(jnp.int32)
        lengthwise, crosswise = Lane(), Lane()
        for b, (a0, a1) in enumerate(spans):
            own = batches[b]
            if group < groups - 1:
                own = lax.ppermute(own, ("rows", "section"), pairs(0, 0, group + 1, group))
            line = [own]
            crossed = [crosswise.send(own, pairs(0, c, group, group)) for c in range(1, minor)]
            for by in shifts[1:]:
                line.append(lengthwise.send(own, pairs(by, 0, group, group)))
            for value in line[1:]:
                crossed += [crosswise.send(value, pairs(0, c, group, group)) for c in range(1, minor)]
            line_order = [((z - by) % major) * minor + y for by in shifts]
            crossed_order = [
                ((z - by) % major) * minor + (y - c) % minor for by in shifts for c in range(1, minor)
            ]
            batch_charge = charge[:, a0:a1]

            def table(order):
                return jnp.stack([live] + [jnp.asarray(i, jnp.int32) for i in order])

            (total,) = part(table(line_order), kernel, gains, batch_charge, line, None, None, a0, False)
            batches[b], result = part(
                table(crossed_order), kernel, gains, batch_charge, crossed, total, result, a0, True
            )
    return result


def solution(mesh):
    return jax.shard_map(
        shards,
        mesh=mesh,
        in_specs=(
            P(("region", "section"), None, "rows", None),
            P(("region", "section"), None, "rows"),
            P(("region", "section"), None, None),
            P("region"),
            P(("region", "rows"), None),
        ),
        out_specs=P(("region", "section"), "rows", None),
        check_vma=False,
    )
```

```python
import functools

import jax
import jax.numpy as jnp
from jax import lax
from jax.experimental import pallas as pl
from jax.experimental.pallas import tpu as pltpu
from jax.sharding import PartitionSpec as P

CHAINS = 2
EARLY = 3
GATES = {3: ((1, ("late", 0)),), 4: ((0, ("late", 1)), (1, ("step", 1)))}
COST = 12
VMEM_LIMIT = 34 * 1024 * 1024


def split(x):
    high = x.astype(jnp.bfloat16)
    return high, (x - high.astype(jnp.float32)).astype(jnp.bfloat16)


def step_kernel(section, steps, who, first, chain, tile, names, info, *refs):
    at = dict(zip(names, refs))
    kernels = [at["own"], at.get("other")]
    blocks = [ref for name, ref in zip(names, refs) if name == "block"]
    x_high, x_low, tiles, t_sem = refs[len(names) :]
    at["token"][...] = jnp.zeros_like(at["token"])
    final = chain is not None
    actions, rows, _ = at["own"].shape
    depth, chain_width = blocks[0].shape
    width = x_high.shape[1]
    per_step = width // chain_width
    count = len(steps)
    tile_count = rows // tile
    lanes = pl.ds(chain * width if final else 0, width)

    def copies(t, slot, source):
        here = pl.ds(pl.multiple_of(t * tile, tile), tile)
        return [
            pltpu.make_async_copy(
                source.at[:, here, pl.ds(pl.multiple_of(info[1 + step] * depth, depth), depth)],
                tiles.at[slot, :, :, pl.ds(i * depth, depth)],
                t_sem.at[slot, i],
            )
            for i, step in enumerate(steps)
        ]

    def fetch(t, slot):
        def start(source):
            for copy in copies(t, slot, source):
                copy.start()

        if who == "own" or who == "other":
            start(kernels[who == "other"])
        else:
            pl.when(info[0] == section)(lambda: start(kernels[0]))
            pl.when(info[0] != section)(lambda: start(kernels[1]))

    def work():
        fetch(0, 0)
        for j, block in enumerate(blocks):
            here = (
                pl.ds(j // per_step * depth, depth),
                pl.ds(j % per_step * chain_width, chain_width),
            )
            x_high[here], x_low[here] = split(block[...])

        @pl.loop(0, tile_count)
        def _(t):
            slot = lax.rem(t, 2)
            here = pl.ds(pl.multiple_of(t * tile, tile), tile)

            @pl.when(t + 1 < tile_count)
            def _():
                fetch(t + 1, 1 - slot)

            for copy in copies(t, slot, kernels[0]):
                copy.wait()
            high, low = split(tiles[slot].reshape(actions * tile, count * depth))
            dot = functools.partial(jnp.dot, preferred_element_type=jnp.float32)
            summed = dot(high, x_high[...]) + (dot(high, x_low[...]) + dot(low, x_high[...]))
            summed = summed.reshape(actions, tile, width)
            if not first:
                summed = summed + at["total"][:, here, lanes]
            if final:
                gains = at["gains"][here, :]
                best = None
                for a in range(actions):
                    value = summed[a] + gains[:, a : a + 1] - at["charge"][a : a + 1, :]
                    best = value if best is None else jnp.maximum(best, value)
                at["values"][here, :] = best
            else:
                at["sum"][:, here, :] = summed

    if who == "all":
        work()
    else:
        pl.when((info[0] == section) if who == "own" else (info[0] != section))(work)


def step(info, section, steps, who, own, other, blocks, total, first, held, chain=None, gains=None, charge=None):
    final = chain is not None
    actions, rows, _ = own.shape
    depth, chain_width = blocks[0].shape
    width = chain_width * len(blocks) // len(steps)
    tile = min(rows, 128)
    hbm = pl.BlockSpec(memory_space=pl.ANY)
    vmem = pl.BlockSpec(memory_space=pltpu.VMEM)
    named = [("own", own, hbm)]
    if other is not None:
        named.append(("other", other, hbm))
    named += [("block", block, vmem) for block in blocks]
    named += [("held", token, vmem) for token in held]
    if final:
        named += [("gains", gains, vmem), ("charge", charge, vmem)]
    aliases = {}
    if total is not None:
        if not final:
            aliases = {1 + len(named): 0}
        named.append(("total", total, vmem))
    if final:
        out = jax.ShapeDtypeStruct((rows, width), jnp.float32)
    else:
        out = jax.ShapeDtypeStruct((actions, rows, width), jnp.float32)
    names = [name for name, _, _ in named] + ["values" if final else "sum", "token"]
    return pl.pallas_call(
        functools.partial(step_kernel, section, steps, who, first, chain, tile, names),
        out_shape=(out, jax.ShapeDtypeStruct((8, 128), jnp.float32)),
        in_specs=[pl.BlockSpec(memory_space=pltpu.SMEM)] + [spec for _, _, spec in named],
        out_specs=(vmem, vmem),
        scratch_shapes=[
            pltpu.VMEM((len(steps) * depth, width), jnp.bfloat16),
            pltpu.VMEM((len(steps) * depth, width), jnp.bfloat16),
            pltpu.VMEM((2, actions, tile, len(steps) * depth), jnp.float32),
            pltpu.SemaphoreType.DMA((2, len(steps))),
        ],
        input_output_aliases=aliases,
        compiler_params=pltpu.CompilerParams(vmem_limit_bytes=VMEM_LIMIT),
        cost_estimate=pl.CostEstimate(
            flops=COST * actions * rows * len(steps) * depth * width,
            bytes_accessed=4 * actions * rows * len(steps) * depth,
            transcendentals=0,
        ),
        name="step",
    )(info, *[value for _, value, _ in named])


def assemble(info, mine, theirs):
    (rows, width), count = mine[0][0].shape, len(mine[0])
    refs = [*mine[0], *mine[1], *theirs[0], *theirs[1]]

    def body(info, *rest):
        ins, out, sem = rest[: 4 * count], rest[-2], rest[-1]

        def copies(core):
            here = ins[core * count : (core + 1) * count]
            there = ins[(2 + core) * count : (3 + core) * count]
            columns = (here + there) if core == 0 else (there + here)
            return [
                pltpu.make_async_copy(ref, out.at[0, :, pl.ds(j * width, width)], sem.at[j])
                for j, ref in enumerate(columns)
            ]

        for core in range(2):

            @pl.when(info[0] == core)
            def _():
                for copy in copies(core):
                    copy.start()
                for copy in copies(core):
                    copy.wait()

    return pl.pallas_call(
        body,
        out_shape=jax.ShapeDtypeStruct((1, rows, 2 * count * width), jnp.float32),
        in_specs=[pl.BlockSpec(memory_space=pltpu.SMEM)] + [pl.BlockSpec(memory_space=pltpu.VMEM)] * len(refs),
        out_specs=pl.BlockSpec(memory_space=pl.ANY),
        scratch_shapes=[pltpu.SemaphoreType.DMA((2 * count,))],
        name="assemble",
    )(info, *refs)


def shards(transitions, gain, cost, price_class, terminal):
    core = lax.axis_index("section")
    row_count = lax.axis_size("rows")
    minor = 2 if row_count == 8 else 1
    major = row_count // minor

    def row_at(place):
        if minor == 1:
            return place
        down = place // major
        return (down * (2 * major - 1) + place * (1 - 2 * down)) * minor + down

    ring = [row_at(i) for i in range(row_count)]
    after = {ring[i]: ring[(i + 1) % row_count] for i in range(row_count)}
    before = {b: a for a, b in after.items()}
    onward = [(r * 2 + 1, after[r] * 2 + 1) for r in range(row_count)]
    onward += [(r * 2, before[r] * 2) for r in range(row_count)]
    swap = [(r * 2 + s, r * 2 + 1 - s) for r in range(row_count) for s in range(2)]

    def send(value, pairs):
        return lax.ppermute(value, ("rows", "section"), pairs)

    own = transitions[0]
    scenarios = terminal.shape[1]
    width = scenarios // 2 // CHAINS
    small = jnp.concatenate([gain[0], cost[0]], axis=1)
    small_other = send(small, swap)
    other = send(lax.optimization_barrier((own, small_other))[0], swap)
    chains = [
        lax.dynamic_slice_in_dim(terminal, core * (scenarios // 2) + i * width, width, 1) for i in range(CHAINS)
    ]

    me = lax.axis_index("rows")
    down = me % minor
    place = down * (2 * major - 1) + (me // minor) * (1 - 2 * down)
    back = jnp.arange(row_count, dtype=jnp.int32) * (1 - 2 * core)
    info = jnp.concatenate([core[None].astype(jnp.int32), row_at((place + back) % row_count).astype(jnp.int32)])

    my_class = lax.dynamic_slice_in_dim(price_class, core * (scenarios // 2), scenarios // 2, 0)
    levels = jnp.arange(cost.shape[2], dtype=jnp.int32)
    onehot = my_class[None, :] == levels[:, None]

    last = row_count - 1
    early = min(EARLY, last // 2)
    groups = [tuple(range(i, min(i + 2, early))) for i in range(0, early, 2)]
    done = [None, None]
    for section in (1, 0):
        here = jnp.where(core == section, small, small_other)
        gains = here[:, : gain.shape[2]].T
        charge = jnp.sum(jnp.where(onehot[None], here[:, gain.shape[2] :, None], 0.0), axis=1)
        total, arrived, tokens, passed = None, [], {}, []

        def add(steps, who, total, first):
            blocks = [block for s in steps for block in arrived[s]]
            held = [passed.pop() for _ in range(len(passed))]
            return step(info, section, steps, who, own, None if who == "own" else other, blocks, total, first, held)

        for s in range(row_count):
            if s:
                gates = GATES.get(s - early, ()) if section == 1 else ()
                for i, gate in gates:
                    if gate in tokens:
                        chains[i], token = lax.optimization_barrier((chains[i], tokens[gate]))
                        passed.append(token)
                chains = [send(chain, onward) for chain in chains]
            arrived.append(list(chains))
            if s == last:
                break
            if section == 1 and s < early:
                total, _ = add((s,), "own", total, s == 0)
                continue
            if section == 1 and s < early + len(groups):
                total, tokens["late", s - early] = add(groups[s - early], "other", total, s == early)
            total, tokens["step", s - early] = add((s,), "all", total, s == 0)
        chains = [
            step(
                info, section, (last,), "all", own, other, [chain], total, False, [], i,
                gains, charge[:, i * width : (i + 1) * width],
            )[0]
            for i, chain in enumerate(chains)
        ]
        done[section] = chains

    across = [[(r * 2 + 1 - c, r * 2 + c) for r in range(row_count)] for c in range(2)]
    received = [[send(value, across[section]) for value in done[section]] for section in range(2)]
    return assemble(info, done, received)


def solution(mesh):
    return jax.shard_map(
        shards,
        mesh=mesh,
        in_specs=(
            P(("region", "section"), None, "rows", None),
            P(("region", "section"), None, "rows"),
            P(("region", "section"), None, None),
            P("region"),
            P(("region", "rows"), None),
        ),
        out_specs=P(("region", "section"), "rows", None),
        check_vma=False,
    )
```

```python
import functools

import jax
import jax.numpy as jnp
from jax import lax
from jax.experimental import pallas as pl
from jax.experimental.pallas import tpu as pltpu
from jax.sharding import PartitionSpec as P

CHAINS = 2
EARLY = 3
PAIR = 2
COST = 12
VMEM_LIMIT = 26 * 1024 * 1024


def split(x):
    high = x.astype(jnp.bfloat16)
    return high, (x - high.astype(jnp.float32)).astype(jnp.bfloat16)


def step_kernel(section, steps, who, first, finish, tile, names, info, *refs):
    at = dict(zip(names, refs))
    kernels = [at["own"], at.get("other")]
    blocks = [ref for name, ref in zip(names, refs) if name == "block"]
    x_high, x_low, tiles, t_sem = refs[len(names) :]
    at["token"][...] = jnp.zeros_like(at["token"])
    final = bool(finish)
    half = CHAINS * blocks[0].shape[1]
    actions, rows, _ = at["own"].shape
    depth, chain_width = blocks[0].shape
    width = x_high.shape[1]
    per_step = width // chain_width
    count = len(steps)
    tile_count = rows // tile
    lanes = pl.ds(finish[0] * width if final else 0, width)

    def copies(t, slot, source):
        here = pl.ds(pl.multiple_of(t * tile, tile), tile)
        return [
            pltpu.make_async_copy(
                source.at[:, here, pl.ds(pl.multiple_of(info[1 + step] * depth, depth), depth)],
                tiles.at[slot, :, :, pl.ds(i * depth, depth)],
                t_sem.at[slot, i],
            )
            for i, step in enumerate(steps)
        ]

    def fetch(t, slot):
        def start(source):
            for copy in copies(t, slot, source):
                copy.start()

        if who == "own" or who == "other":
            start(kernels[who == "other"])
        else:
            pl.when(info[0] == section)(lambda: start(kernels[0]))
            pl.when(info[0] != section)(lambda: start(kernels[1]))

    def work():
        fetch(0, 0)
        for j, block in enumerate(blocks):
            here = (
                pl.ds(j // per_step * depth, depth),
                pl.ds(j % per_step * chain_width, chain_width),
            )
            x_high[here], x_low[here] = split(block[...])

        @pl.loop(0, tile_count)
        def _(t):
            slot = lax.rem(t, 2)
            here = pl.ds(pl.multiple_of(t * tile, tile), tile)

            @pl.when(t + 1 < tile_count)
            def _():
                fetch(t + 1, 1 - slot)

            for copy in copies(t, slot, kernels[0]):
                copy.wait()
            high, low = split(tiles[slot].reshape(actions * tile, count * depth))
            dot = functools.partial(jnp.dot, preferred_element_type=jnp.float32)
            summed = dot(high, x_high[...]) + (dot(high, x_low[...]) + dot(low, x_high[...]))
            summed = summed.reshape(actions, tile, width)
            if not first:
                summed = summed + at["total"][:, here, lanes]
            if final:
                mine = info[0] == section
                gains = jnp.where(mine, at["gains", 0][here, :], at["gains", 1][here, :])
                columns = pl.ds(pl.multiple_of(info[0] * half + finish[0] * chain_width, chain_width), width)
                charge = jnp.where(mine, at["charge", 0][:, columns], at["charge", 1][:, columns])
                best = None
                for a in range(actions):
                    value = summed[a] + gains[:, a : a + 1] - charge[a : a + 1, :]
                    best = value if best is None else jnp.maximum(best, value)
                for i, chain in enumerate(finish):
                    at["values", chain][here, :] = best[:, i * chain_width : (i + 1) * chain_width]
            else:
                at["sum"][:, here, :] = summed

    if who == "all":
        work()
    else:
        pl.when((info[0] == section) if who == "own" else (info[0] != section))(work)


def step(info, section, steps, who, own, other, blocks, total, first, held, finish=(), terms=()):
    final = bool(finish)
    actions, rows, _ = own.shape
    depth, chain_width = blocks[0].shape
    width = chain_width * len(blocks) // len(steps)
    tile = min(rows, 128)
    hbm = pl.BlockSpec(memory_space=pl.ANY)
    vmem = pl.BlockSpec(memory_space=pltpu.VMEM)
    named = [("own", own, pl.BlockSpec(memory_space=pltpu.HBM))]
    if other is not None:
        named.append(("other", other, pl.BlockSpec(memory_space=pltpu.HBM)))
    named += [("block", block, vmem) for block in blocks]
    named += [("held", token, vmem) for token in held]
    if final:
        names = (("gains", 0), ("charge", 0), ("gains", 1), ("charge", 1))
        named += [(name, term, vmem) for name, term in zip(names, terms)]
    aliases = {}
    if total is not None:
        if not final:
            aliases = {1 + len(named): 0}
        named.append(("total", total, vmem))
    if final:
        outs = [jax.ShapeDtypeStruct((rows, chain_width), jnp.float32) for _ in finish]
        out_names = [("values", chain) for chain in finish]
    else:
        outs, out_names = [jax.ShapeDtypeStruct((actions, rows, width), jnp.float32)], ["sum"]
    names = [name for name, _, _ in named] + out_names + ["token"]
    return pl.pallas_call(
        functools.partial(step_kernel, section, steps, who, first, tuple(finish), tile, names),
        out_shape=(*outs, jax.ShapeDtypeStruct((8, 128), jnp.float32)),
        in_specs=[pl.BlockSpec(memory_space=pltpu.SMEM)] + [spec for _, _, spec in named],
        out_specs=tuple([vmem] * (len(outs) + 1)),
        scratch_shapes=[
            pltpu.VMEM((len(steps) * depth, width), jnp.bfloat16),
            pltpu.VMEM((len(steps) * depth, width), jnp.bfloat16),
            pltpu.VMEM((2, actions, tile, len(steps) * depth), jnp.float32),
            pltpu.SemaphoreType.DMA((2, len(steps))),
        ],
        input_output_aliases=aliases,
        compiler_params=pltpu.CompilerParams(vmem_limit_bytes=VMEM_LIMIT),
        cost_estimate=pl.CostEstimate(
            flops=COST * actions * rows * len(steps) * depth * width,
            bytes_accessed=4 * actions * rows * len(steps) * depth,
            transcendentals=0,
        ),
        name="step",
    )(info, *[value for _, value, _ in named])


def assemble(info, mine, theirs, ready, result):
    rows, width = mine[0][0].shape
    chosen = [
        (core, (core * CHAINS + i if there == 0 else (1 - core) * CHAINS + i), (theirs if there else mine)[core][i])
        for core in range(2)
        for i in ready[core]
        for there in range(2)
    ]
    refs = [value for _, _, value in chosen]
    aliases = {} if result is None else {1 + len(refs): 0}

    def body(info, *rest):
        ins, out, sem = rest[: len(refs)], rest[-2], rest[-1]
        for core in range(2):

            @pl.when(info[0] == core)
            def _():
                copies = [
                    pltpu.make_async_copy(ref, out.at[0, :, pl.ds(place * width, width)], sem.at[j])
                    for j, (ref, (owner, place, _)) in enumerate(zip(ins, chosen))
                    if owner == core
                ]
                for copy in copies:
                    copy.start()
                for copy in copies:
                    copy.wait()

    hbm = pl.BlockSpec(memory_space=pl.ANY)
    return pl.pallas_call(
        body,
        out_shape=jax.ShapeDtypeStruct((1, rows, 2 * CHAINS * width), jnp.float32),
        in_specs=[pl.BlockSpec(memory_space=pltpu.SMEM)]
        + [pl.BlockSpec(memory_space=pltpu.VMEM)] * len(refs)
        + [hbm] * len(aliases),
        out_specs=hbm,
        scratch_shapes=[pltpu.SemaphoreType.DMA((len(refs),))],
        input_output_aliases=aliases,
        name="assemble",
    )(info, *refs, *([] if result is None else [result]))


def shards(transitions, gain, cost, price_class, terminal):
    core = lax.axis_index("section")
    row_count = lax.axis_size("rows")
    minor = 2 if row_count == 8 else 1
    major = row_count // minor

    def row_at(place):
        if minor == 1:
            return place
        down = place // major
        return (down * (2 * major - 1) + place * (1 - 2 * down)) * minor + down

    ring = [row_at(i) for i in range(row_count)]
    after = {ring[i]: ring[(i + 1) % row_count] for i in range(row_count)}
    before = {b: a for a, b in after.items()}
    onward = [(r * 2 + 1, after[r] * 2 + 1) for r in range(row_count)]
    onward += [(r * 2, before[r] * 2) for r in range(row_count)]
    swap = [(r * 2 + s, r * 2 + 1 - s) for r in range(row_count) for s in range(2)]

    def send(value, pairs):
        return lax.ppermute(value, ("rows", "section"), pairs)

    own = transitions[0]
    scenarios = terminal.shape[1]
    width = scenarios // 2 // CHAINS
    chains = [
        lax.dynamic_slice_in_dim(terminal, core * (scenarios // 2) + i * width, width, 1) for i in range(CHAINS)
    ]

    me = lax.axis_index("rows")
    down = me % minor
    place = down * (2 * major - 1) + (me // minor) * (1 - 2 * down)
    back = jnp.arange(row_count, dtype=jnp.int32) * (1 - 2 * core)
    info = jnp.concatenate([core[None].astype(jnp.int32), row_at((place + back) % row_count).astype(jnp.int32)])

    levels = jnp.arange(cost.shape[2], dtype=jnp.int32)
    onehot = price_class[None, :] == levels[:, None]
    other = send(own, swap)
    terms = [gain[0].T, jnp.sum(jnp.where(onehot[None], cost[0][:, :, None], 0.0), axis=1)]

    last = row_count - 1
    groups = [tuple(range(i, min(i + PAIR, last - 1))) for i in range(0, last - 1, PAIR)]
    when = {max(EARLY + i, group[-1]): [group] for i, group in enumerate(groups)}
    when[last - 2] = [(step,) for group in when[last - 2] for step in group]
    done = [None, None]
    for section in (1, 0):
        total, arrived, tokens, passed = None, [], {}, []

        def add(steps, who, total, first):
            blocks = [block for s in steps for block in arrived[s]]
            held = [passed.pop() for _ in range(len(passed))]
            return step(info, section, steps, who, own, None if who == "own" else other, blocks, total, first, held)

        for s in range(row_count):
            if s:
                for i, gate in ((0, s - 3), (-1, s - 2)):
                    if gate in tokens:
                        chains[i], tokens[gate] = lax.optimization_barrier((chains[i], tokens[gate]))
                        if i == 0 or s == last:
                            passed.append(tokens[gate])
                chains = [send(chain, onward) for chain in chains]
            arrived.append(list(chains))
            if section == 1 and s == 1:
                chains[0], *terms = lax.optimization_barrier((chains[0], *terms))
                terms += [send(term, swap) for term in terms]
            if section == 0 and s < last:
                total, _ = add((s,), "all", total, s == 0)
            if section == 1 and s < last - 1:
                total, _ = add((s,), "own", total, s == 0)
                for group in when.get(s, ()):
                    total, token = add(group, "other", total, group[0] == 0)
                    tokens.setdefault(s, token)
        if section == 1:
            steps = (last - 1, last)
            blocks = arrived[-2] + arrived[-1]
            chains = step(info, section, steps, "all", own, other, blocks, total, False, passed, range(CHAINS), terms)[:CHAINS]
        else:
            chains = [
                step(
                    info, section, (last,), "all", own, other, [chain], total, False, [], (i,), terms
                )[0]
                for i, chain in enumerate(chains)
            ]
        chains = list(chains)
        done[section] = chains

    across = [[(r * 2 + 1 - c, r * 2 + c) for r in range(row_count)] for c in range(2)]
    received = [[send(value, across[section]) for value in done[section]] for section in range(2)]
    result = assemble(info, done, received, (range(CHAINS - 1), range(CHAINS)), None)
    return assemble(info, done, received, ((CHAINS - 1,), ()), result)


def solution(mesh):
    return jax.shard_map(
        shards,
        mesh=mesh,
        in_specs=(
            P(("region", "section"), None, "rows", None),
            P(("region", "section"), None, "rows"),
            P(("region", "section"), None, None),
            P("region"),
            P(("region", "rows"), None),
        ),
        out_specs=P(("region", "section"), "rows", None),
        check_vma=False,
    )
```

```python
import functools

import jax
import jax.numpy as jnp
from jax import lax
from jax.experimental import pallas as pl
from jax.experimental.pallas import tpu as pltpu
from jax.sharding import PartitionSpec as P

CHAINS = 2
EARLY = 3
PAIR = 2
COST = 12
VMEM_LIMIT = 26 * 1024 * 1024


def split(x):
    high = x.astype(jnp.bfloat16)
    return high, (x - high.astype(jnp.float32)).astype(jnp.bfloat16)


def step_kernel(section, steps, who, first, finish, tile, names, info, *refs):
    at = dict(zip(names, refs))
    kernels = [at["own"], at.get("other")]
    blocks = [ref for name, ref in zip(names, refs) if name == "block"]
    x_high, x_low, tiles, t_sem = refs[len(names) :]
    at["token"][...] = jnp.zeros_like(at["token"])
    final = bool(finish)
    half = CHAINS * blocks[0].shape[1]
    actions, rows, _ = at["own"].shape
    depth, chain_width = blocks[0].shape
    width = x_high.shape[1]
    per_step = width // chain_width
    count = len(steps)
    tile_count = rows // tile
    lanes = pl.ds(finish[0] * width if final else 0, width)

    def copies(t, slot, source):
        here = pl.ds(pl.multiple_of(t * tile, tile), tile)
        return [
            pltpu.make_async_copy(
                source.at[:, here, pl.ds(pl.multiple_of(info[1 + step] * depth, depth), depth)],
                tiles.at[slot, :, :, pl.ds(i * depth, depth)],
                t_sem.at[slot, i],
            )
            for i, step in enumerate(steps)
        ]

    def fetch(t, slot):
        def start(source):
            for copy in copies(t, slot, source):
                copy.start()

        if who == "own" or who == "other":
            start(kernels[who == "other"])
        else:
            pl.when(info[0] == section)(lambda: start(kernels[0]))
            pl.when(info[0] != section)(lambda: start(kernels[1]))

    def work():
        fetch(0, 0)
        for j, block in enumerate(blocks):
            here = (
                pl.ds(j // per_step * depth, depth),
                pl.ds(j % per_step * chain_width, chain_width),
            )
            x_high[here], x_low[here] = split(block[...])

        @pl.loop(0, tile_count)
        def _(t):
            slot = lax.rem(t, 2)
            here = pl.ds(pl.multiple_of(t * tile, tile), tile)

            @pl.when(t + 1 < tile_count)
            def _():
                fetch(t + 1, 1 - slot)

            for copy in copies(t, slot, kernels[0]):
                copy.wait()
            high, low = split(tiles[slot].reshape(actions * tile, count * depth))
            dot = functools.partial(jnp.dot, preferred_element_type=jnp.float32)
            summed = dot(high, x_high[...]) + (dot(high, x_low[...]) + dot(low, x_high[...]))
            summed = summed.reshape(actions, tile, width)
            if not first:
                summed = summed + at["total"][:, here, lanes]
            if final:
                mine = info[0] == section
                gains = jnp.where(mine, at["gains", 0][here, :], at["gains", 1][here, :])
                columns = pl.ds(pl.multiple_of(info[0] * half + finish[0] * chain_width, chain_width), width)
                charge = jnp.where(mine, at["charge", 0][:, columns], at["charge", 1][:, columns])
                best = None
                for a in range(actions):
                    value = summed[a] + gains[:, a : a + 1] - charge[a : a + 1, :]
                    best = value if best is None else jnp.maximum(best, value)
                for i, chain in enumerate(finish):
                    at["values", chain][here, :] = best[:, i * chain_width : (i + 1) * chain_width]
            else:
                at["sum"][:, here, :] = summed

    if who == "all":
        work()
    else:
        pl.when((info[0] == section) if who == "own" else (info[0] != section))(work)


def step(info, section, steps, who, own, other, blocks, total, first, held, finish=(), terms=()):
    final = bool(finish)
    actions, rows, _ = own.shape
    depth, chain_width = blocks[0].shape
    width = chain_width * len(blocks) // len(steps)
    tile = min(rows, 128)
    hbm = pl.BlockSpec(memory_space=pl.ANY)
    vmem = pl.BlockSpec(memory_space=pltpu.VMEM)
    named = [("own", own, pl.BlockSpec(memory_space=pltpu.HBM))]
    if other is not None:
        named.append(("other", other, pl.BlockSpec(memory_space=pltpu.HBM)))
    named += [("block", block, vmem) for block in blocks]
    named += [("held", token, vmem) for token in held]
    if final:
        names = (("gains", 0), ("charge", 0), ("gains", 1), ("charge", 1))
        named += [(name, term, vmem) for name, term in zip(names, terms)]
    aliases = {}
    if total is not None:
        if not final:
            aliases = {1 + len(named): 0}
        named.append(("total", total, vmem))
    if final:
        outs = [jax.ShapeDtypeStruct((rows, chain_width), jnp.float32) for _ in finish]
        out_names = [("values", chain) for chain in finish]
    else:
        outs, out_names = [jax.ShapeDtypeStruct((actions, rows, width), jnp.float32)], ["sum"]
    names = [name for name, _, _ in named] + out_names + ["token"]
    return pl.pallas_call(
        functools.partial(step_kernel, section, steps, who, first, tuple(finish), tile, names),
        out_shape=(*outs, jax.ShapeDtypeStruct((8, 128), jnp.float32)),
        in_specs=[pl.BlockSpec(memory_space=pltpu.SMEM)] + [spec for _, _, spec in named],
        out_specs=tuple([vmem] * (len(outs) + 1)),
        scratch_shapes=[
            pltpu.VMEM((len(steps) * depth, width), jnp.bfloat16),
            pltpu.VMEM((len(steps) * depth, width), jnp.bfloat16),
            pltpu.VMEM((2, actions, tile, len(steps) * depth), jnp.float32),
            pltpu.SemaphoreType.DMA((2, len(steps))),
        ],
        input_output_aliases=aliases,
        compiler_params=pltpu.CompilerParams(vmem_limit_bytes=VMEM_LIMIT),
        cost_estimate=pl.CostEstimate(
            flops=COST * actions * rows * len(steps) * depth * width,
            bytes_accessed=4 * actions * rows * len(steps) * depth,
            transcendentals=0,
        ),
        name="step",
    )(info, *[value for _, value, _ in named])


def assemble(info, mine, theirs, ready, result):
    rows, width = mine[0][0].shape
    chosen = [
        (core, (core * CHAINS + i if there == 0 else (1 - core) * CHAINS + i), (theirs if there else mine)[core][i])
        for core, there, i in ready
    ]
    refs = [value for _, _, value in chosen]
    aliases = {} if result is None else {1 + len(refs): 0}

    def body(info, *rest):
        ins, out, sem = rest[: len(refs)], rest[-2], rest[-1]
        for core in range(2):

            @pl.when(info[0] == core)
            def _():
                copies = [
                    pltpu.make_async_copy(ref, out.at[0, :, pl.ds(place * width, width)], sem.at[j])
                    for j, (ref, (owner, place, _)) in enumerate(zip(ins, chosen))
                    if owner == core
                ]
                for copy in copies:
                    copy.start()
                for copy in copies:
                    copy.wait()

    hbm = pl.BlockSpec(memory_space=pl.ANY)
    return pl.pallas_call(
        body,
        out_shape=jax.ShapeDtypeStruct((1, rows, 2 * CHAINS * width), jnp.float32),
        in_specs=[pl.BlockSpec(memory_space=pltpu.SMEM)]
        + [pl.BlockSpec(memory_space=pltpu.VMEM)] * len(refs)
        + [hbm] * len(aliases),
        out_specs=hbm,
        scratch_shapes=[pltpu.SemaphoreType.DMA((len(refs),))],
        input_output_aliases=aliases,
        compiler_params=pltpu.CompilerParams(vmem_limit_bytes=8 * 1024 * 1024),
        name="assemble",
    )(info, *refs, *([] if result is None else [result]))


def shards(transitions, gain, cost, price_class, terminal):
    core = lax.axis_index("section")
    row_count = lax.axis_size("rows")
    minor = 2 if row_count == 8 else 1
    major = row_count // minor

    def row_at(place):
        if minor == 1:
            return place
        down = place // major
        return (down * (2 * major - 1) + place * (1 - 2 * down)) * minor + down

    ring = [row_at(i) for i in range(row_count)]
    after = {ring[i]: ring[(i + 1) % row_count] for i in range(row_count)}
    before = {b: a for a, b in after.items()}
    onward = [(r * 2 + 1, after[r] * 2 + 1) for r in range(row_count)]
    onward += [(r * 2, before[r] * 2) for r in range(row_count)]
    swap = [(r * 2 + s, r * 2 + 1 - s) for r in range(row_count) for s in range(2)]

    def send(value, pairs):
        return lax.ppermute(value, ("rows", "section"), pairs)

    own = transitions[0]
    scenarios = terminal.shape[1]
    width = scenarios // 2 // CHAINS
    chains = [
        lax.dynamic_slice_in_dim(terminal, core * (scenarios // 2) + i * width, width, 1) for i in range(CHAINS)
    ]

    me = lax.axis_index("rows")
    down = me % minor
    place = down * (2 * major - 1) + (me // minor) * (1 - 2 * down)
    back = jnp.arange(row_count, dtype=jnp.int32) * (1 - 2 * core)
    info = jnp.concatenate([core[None].astype(jnp.int32), row_at((place + back) % row_count).astype(jnp.int32)])

    levels = jnp.arange(cost.shape[2], dtype=jnp.int32)
    onehot = price_class[None, :] == levels[:, None]
    other = send(own, swap)
    terms = [gain[0].T, jnp.sum(jnp.where(onehot[None], cost[0][:, :, None], 0.0), axis=1)]

    last = row_count - 1
    groups = [tuple(range(i, min(i + PAIR, last - 1))) for i in range(0, last - 1, PAIR)]
    when = {max(EARLY + i, group[-1]): [group] for i, group in enumerate(groups)}
    when[last - 2] = [(step,) for group in when[last - 2] for step in group]
    across = [[(r * 2 + 1 - c, r * 2 + c) for r in range(row_count)] for c in range(2)]
    received = [[], []]
    done = [None, None]
    for section in (1, 0):
        total, arrived, tokens, passed = None, [], {}, []

        def add(steps, who, total, first):
            blocks = [block for s in steps for block in arrived[s]]
            held = [passed.pop() for _ in range(len(passed))]
            return step(info, section, steps, who, own, None if who == "own" else other, blocks, total, first, held)

        for s in range(row_count):
            if s:
                for i, gate in ((0, s - 3), (-1, s - 2)):
                    if gate in tokens:
                        chains[i], tokens[gate] = lax.optimization_barrier((chains[i], tokens[gate]))
                        if i == 0 or s == last:
                            passed.append(tokens[gate])
                chains = [send(chain, onward) for chain in chains]
            arrived.append(list(chains))
            if section == 1 and s == 1:
                chains[0], *terms = lax.optimization_barrier((chains[0], *terms))
                terms += [send(term, swap) for term in terms]
            if section == 0 and s < last:
                total, token = add((s,), "all", total, s == 0)
                if 0 < s <= CHAINS:
                    value, token = lax.optimization_barrier((done[1][s - 1], token))
                    passed.append(token)
                    received[1].append(send(value, across[1]))
            if section == 1 and s < last - 1:
                total, _ = add((s,), "own", total, s == 0)
                for group in when.get(s, ()):
                    total, token = add(group, "other", total, group[0] == 0)
                    tokens.setdefault(s, token)
        if section == 1:
            steps = (last - 1, last)
            blocks = arrived[-2] + arrived[-1]
            chains = step(info, section, steps, "all", own, other, blocks, total, False, passed, range(CHAINS), terms)[:CHAINS]
        else:
            chains = [
                step(
                    info, section, (last,), "all", own, other, [chain], total, False, [], (i,), terms
                )[0]
                for i, chain in enumerate(chains)
            ]
        chains = list(chains)
        done[section] = chains

    received[0] = [send(value, across[0]) for value in done[0]]
    ready = [(c, there, i) for c in range(2) for there in range(2) for i in range(CHAINS)]
    late = (0, 1, CHAINS - 1)
    result = assemble(info, done, received, [chunk for chunk in ready if chunk != late], None)
    return assemble(info, done, received, [late], result)


def solution(mesh):
    return jax.shard_map(
        shards,
        mesh=mesh,
        in_specs=(
            P(("region", "section"), None, "rows", None),
            P(("region", "section"), None, "rows"),
            P(("region", "section"), None, None),
            P("region"),
            P(("region", "rows"), None),
        ),
        out_specs=P(("region", "section"), "rows", None),
        check_vma=False,
    )
```

```python
import functools

import jax
import jax.numpy as jnp
from jax import lax
from jax.experimental import pallas as pl
from jax.experimental.pallas import tpu as pltpu
from jax.sharding import PartitionSpec as P

CHAINS = 2
EARLY = 3
SLOTS = 3
PAIR = 2
COST = 12
VMEM_LIMIT = 26 * 1024 * 1024


def split(x):
    high = x.astype(jnp.bfloat16)
    return high, (x - high.astype(jnp.float32)).astype(jnp.bfloat16)


def step_kernel(section, steps, who, first, finish, tile, names, info, *refs):
    at = dict(zip(names, refs))
    kernels = [at["own"], at.get("other")]
    blocks = [ref for name, ref in zip(names, refs) if name == "block"]
    x_high, x_low, tiles, t_sem = refs[len(names) :]
    at["token"][...] = jnp.zeros_like(at["token"])
    final = bool(finish)
    half = CHAINS * blocks[0].shape[1]
    actions, rows, _ = at["own"].shape
    depth, chain_width = blocks[0].shape
    width = x_high.shape[1]
    per_step = width // chain_width
    count = len(steps)
    tile_count, slots = rows // tile, tiles.shape[0]
    lanes = pl.ds(finish[0] * width if final else 0, width)

    def copies(t, slot, source):
        here = pl.ds(pl.multiple_of(t * tile, tile), tile)
        parts = 1 if count > 1 else actions
        share = actions // parts
        return [
            pltpu.make_async_copy(
                source.at[
                    pl.ds(a * share, share), here, pl.ds(pl.multiple_of(info[1 + step] * depth, depth), depth)
                ],
                tiles.at[slot, pl.ds(a * share, share), :, pl.ds(i * depth, depth)],
                t_sem.at[slot, i, a],
            )
            for i, step in enumerate(steps)
            for a in range(parts)
        ]

    def fetch(t, slot):
        def start(source):
            for copy in copies(t, slot, source):
                copy.start()

        if who == "own" or who == "other":
            start(kernels[who == "other"])
        else:
            pl.when(info[0] == section)(lambda: start(kernels[0]))
            pl.when(info[0] != section)(lambda: start(kernels[1]))

    def work():
        for t in range(min(slots - 1, tile_count)):
            fetch(t, t)
        for j, block in enumerate(blocks):
            here = (
                pl.ds(j // per_step * depth, depth),
                pl.ds(j % per_step * chain_width, chain_width),
            )
            x_high[here], x_low[here] = split(block[...])

        @pl.loop(0, tile_count)
        def _(t):
            slot = lax.rem(t, slots)
            here = pl.ds(pl.multiple_of(t * tile, tile), tile)

            @pl.when(t + slots - 1 < tile_count)
            def _():
                fetch(t + slots - 1, lax.rem(t + slots - 1, slots))

            for copy in copies(t, slot, kernels[0]):
                copy.wait()
            high, low = split(tiles[slot].reshape(actions * tile, count * depth))
            dot = functools.partial(jnp.dot, preferred_element_type=jnp.float32)
            summed = dot(high, x_high[...]) + (dot(high, x_low[...]) + dot(low, x_high[...]))
            summed = summed.reshape(actions, tile, width)
            if not first:
                summed = summed + at["total"][:, here, lanes]
            if final:
                mine = info[0] == section
                gains = jnp.where(mine, at["gains", 0][here, :], at["gains", 1][here, :])
                columns = pl.ds(pl.multiple_of(info[0] * half + finish[0] * chain_width, chain_width), width)
                charge = jnp.where(mine, at["charge", 0][:, columns], at["charge", 1][:, columns])
                best = None
                for a in range(actions):
                    value = summed[a] + gains[:, a : a + 1] - charge[a : a + 1, :]
                    best = value if best is None else jnp.maximum(best, value)
                for i, chain in enumerate(finish):
                    at["values", chain][here, :] = best[:, i * chain_width : (i + 1) * chain_width]
            else:
                at["sum"][:, here, :] = summed

    if who == "all":
        work()
    else:
        pl.when((info[0] == section) if who == "own" else (info[0] != section))(work)


def step(info, section, steps, who, own, other, blocks, total, first, held, finish=(), terms=()):
    final = bool(finish)
    actions, rows, _ = own.shape
    depth, chain_width = blocks[0].shape
    width = chain_width * len(blocks) // len(steps)
    tile = min(rows, 128)
    slots = SLOTS if len(steps) == 1 else 2
    hbm = pl.BlockSpec(memory_space=pl.ANY)
    vmem = pl.BlockSpec(memory_space=pltpu.VMEM)
    named = [("own", own, pl.BlockSpec(memory_space=pltpu.HBM))]
    if other is not None:
        named.append(("other", other, pl.BlockSpec(memory_space=pltpu.HBM)))
    named += [("block", block, vmem) for block in blocks]
    named += [("held", token, vmem) for token in held]
    if final:
        names = (("gains", 0), ("charge", 0), ("gains", 1), ("charge", 1))
        named += [(name, term, vmem) for name, term in zip(names, terms)]
    aliases = {}
    if total is not None:
        if not final:
            aliases = {1 + len(named): 0}
        named.append(("total", total, vmem))
    if final:
        outs = [jax.ShapeDtypeStruct((rows, chain_width), jnp.float32) for _ in finish]
        out_names = [("values", chain) for chain in finish]
    else:
        outs, out_names = [jax.ShapeDtypeStruct((actions, rows, width), jnp.float32)], ["sum"]
    names = [name for name, _, _ in named] + out_names + ["token"]
    return pl.pallas_call(
        functools.partial(step_kernel, section, steps, who, first, tuple(finish), tile, names),
        out_shape=(*outs, jax.ShapeDtypeStruct((8, 128), jnp.float32)),
        in_specs=[pl.BlockSpec(memory_space=pltpu.SMEM)] + [spec for _, _, spec in named],
        out_specs=tuple([vmem] * (len(outs) + 1)),
        scratch_shapes=[
            pltpu.VMEM((len(steps) * depth, width), jnp.bfloat16),
            pltpu.VMEM((len(steps) * depth, width), jnp.bfloat16),
            pltpu.VMEM((slots, actions, tile, len(steps) * depth), jnp.float32),
            pltpu.SemaphoreType.DMA((slots, len(steps), actions)),
        ],
        input_output_aliases=aliases,
        compiler_params=pltpu.CompilerParams(vmem_limit_bytes=VMEM_LIMIT),
        cost_estimate=pl.CostEstimate(
            flops=COST * actions * rows * len(steps) * depth * width,
            bytes_accessed=4 * actions * rows * len(steps) * depth,
            transcendentals=0,
        ),
        name="step",
    )(info, *[value for _, value, _ in named])


def assemble(info, mine, theirs, ready, result):
    rows, width = mine[0][0].shape
    chosen = [
        (core, (core * CHAINS + i if there == 0 else (1 - core) * CHAINS + i), (theirs if there else mine)[core][i])
        for core, there, i in ready
    ]
    refs = [value for _, _, value in chosen]
    aliases = {} if result is None else {1 + len(refs): 0}

    def body(info, *rest):
        ins, out, sem = rest[: len(refs)], rest[-2], rest[-1]
        for core in range(2):

            @pl.when(info[0] == core)
            def _():
                copies = [
                    pltpu.make_async_copy(ref, out.at[0, :, pl.ds(place * width, width)], sem.at[j])
                    for j, (ref, (owner, place, _)) in enumerate(zip(ins, chosen))
                    if owner == core
                ]
                for copy in copies:
                    copy.start()
                for copy in copies:
                    copy.wait()

    hbm = pl.BlockSpec(memory_space=pl.ANY)
    return pl.pallas_call(
        body,
        out_shape=jax.ShapeDtypeStruct((1, rows, 2 * CHAINS * width), jnp.float32),
        in_specs=[pl.BlockSpec(memory_space=pltpu.SMEM)]
        + [pl.BlockSpec(memory_space=pltpu.VMEM)] * len(refs)
        + [hbm] * len(aliases),
        out_specs=hbm,
        scratch_shapes=[pltpu.SemaphoreType.DMA((len(refs),))],
        input_output_aliases=aliases,
        compiler_params=pltpu.CompilerParams(vmem_limit_bytes=8 * 1024 * 1024),
        name="assemble",
    )(info, *refs, *([] if result is None else [result]))


def shards(transitions, gain, cost, price_class, terminal):
    core = lax.axis_index("section")
    row_count = lax.axis_size("rows")
    minor = 2 if row_count == 8 else 1
    major = row_count // minor

    def row_at(place):
        if minor == 1:
            return place
        down = place // major
        return (down * (2 * major - 1) + place * (1 - 2 * down)) * minor + down

    ring = [row_at(i) for i in range(row_count)]
    after = {ring[i]: ring[(i + 1) % row_count] for i in range(row_count)}
    before = {b: a for a, b in after.items()}
    onward = [(r * 2 + 1, after[r] * 2 + 1) for r in range(row_count)]
    onward += [(r * 2, before[r] * 2) for r in range(row_count)]
    swap = [(r * 2 + s, r * 2 + 1 - s) for r in range(row_count) for s in range(2)]

    def send(value, pairs):
        return lax.ppermute(value, ("rows", "section"), pairs)

    own = transitions[0]
    scenarios = terminal.shape[1]
    width = scenarios // 2 // CHAINS
    chains = [
        lax.dynamic_slice_in_dim(terminal, core * (scenarios // 2) + i * width, width, 1) for i in range(CHAINS)
    ]

    me = lax.axis_index("rows")
    down = me % minor
    place = down * (2 * major - 1) + (me // minor) * (1 - 2 * down)
    back = jnp.arange(row_count, dtype=jnp.int32) * (1 - 2 * core)
    info = jnp.concatenate([core[None].astype(jnp.int32), row_at((place + back) % row_count).astype(jnp.int32)])

    levels = jnp.arange(cost.shape[2], dtype=jnp.int32)
    onehot = price_class[None, :] == levels[:, None]
    other = send(own, swap)
    terms = [gain[0].T, jnp.sum(jnp.where(onehot[None], cost[0][:, :, None], 0.0), axis=1)]

    last = row_count - 1
    groups = [tuple(range(i, min(i + PAIR, last - 1))) for i in range(0, last - 1, PAIR)]
    when = {max(EARLY + i, group[-1]): [group] for i, group in enumerate(groups)}
    when[last - 2] = [(step,) for group in when[last - 2] for step in group]
    across = [[(r * 2 + 1 - c, r * 2 + c) for r in range(row_count)] for c in range(2)]
    received = [[], []]
    done = [None, None]
    for section in (1, 0):
        total, arrived, tokens, passed = None, [], {}, []

        def add(steps, who, total, first):
            blocks = [block for s in steps for block in arrived[s]]
            held = [passed.pop() for _ in range(len(passed))]
            return step(info, section, steps, who, own, None if who == "own" else other, blocks, total, first, held)

        for s in range(row_count):
            if s:
                for i, gate in ((0, s - 3), (-1, s - 2)):
                    if gate in tokens:
                        chains[i], tokens[gate] = lax.optimization_barrier((chains[i], tokens[gate]))
                        if i == 0 or s == last:
                            passed.append(tokens[gate])
                chains = [send(chain, onward) for chain in chains]
            arrived.append(list(chains))
            if section == 1 and s == 1:
                chains[0], *terms = lax.optimization_barrier((chains[0], *terms))
                terms += [send(term, swap) for term in terms]
            if section == 0 and s < last:
                total, token = add((s,), "all", total, s == 0)
                if 0 < s <= CHAINS:
                    value, token = lax.optimization_barrier((done[1][s - 1], token))
                    passed.append(token)
                    received[1].append(send(value, across[1]))
            if section == 1 and s < last - 1:
                total, _ = add((s,), "own", total, s == 0)
                for group in when.get(s, ()):
                    total, token = add(group, "other", total, group[0] == 0)
                    tokens.setdefault(s, token)
        if section == 1:
            steps = (last - 1, last)
            blocks = arrived[-2] + arrived[-1]
            chains = step(info, section, steps, "all", own, other, blocks, total, False, passed, range(CHAINS), terms)[:CHAINS]
        else:
            chains = [
                step(
                    info, section, (last,), "all", own, other, [chain], total, False, [], (i,), terms
                )[0]
                for i, chain in enumerate(chains)
            ]
        chains = list(chains)
        done[section] = chains

    received[0] = [send(value, across[0]) for value in done[0]]
    ready = [(c, there, i) for c in range(2) for there in range(2) for i in range(CHAINS)]
    late = (0, 1, CHAINS - 1)
    result = assemble(info, done, received, [chunk for chunk in ready if chunk != late], None)
    return assemble(info, done, received, [late], result)


def solution(mesh):
    return jax.shard_map(
        shards,
        mesh=mesh,
        in_specs=(
            P(("region", "section"), None, "rows", None),
            P(("region", "section"), None, "rows"),
            P(("region", "section"), None, None),
            P("region"),
            P(("region", "rows"), None),
        ),
        out_specs=P(("region", "section"), "rows", None),
        check_vma=False,
    )
```
